32 devices in a mesh: dp: 8 (over z, y), fsdp: 4 (over x, core).
Axes of the slice: x: 2, y: 2, z: 4, core: 2. Of those that a mesh axis runs over, the one named last changes fastest.
Arguments:
- tokens: bfloat16 [4096, 960], P(('dp', 'fsdp')), may hold values from -6 to 6
- segment_ids: int32 [64, 64], P(('dp', 'fsdp')), may hold values from 0 to 2, never falling along the last dimension, each value on 1 to 40 neighbouring positions
- w_query: bfloat16 [960, 960], P('dp', 'fsdp'), may hold values from -0.1875 to 0.1875
- w_key: bfloat16 [960, 320], P('dp', 'fsdp'), may hold values from -0.1875 to 0.1875
- w_value: bfloat16 [960, 320], P('dp', 'fsdp'), may hold values from -0.1875 to 0.1875
- w_output: bfloat16 [960, 960], P('dp', 'fsdp'), may hold values from -0.75 to 0.75
- w_gate: bfloat16 [960, 2560], P('dp', 'fsdp'), may hold values from -0.1875 to 0.1875
- w_up: bfloat16 [960, 2560], P('dp', 'fsdp'), may hold values from -0.1875 to 0.1875
- w_down: bfloat16 [2560, 960], P('dp', 'fsdp'), may hold values from -0.125 to 0.125
- gain_attn: bfloat16 [960], P('dp'), may hold values from 0.099609375 to 1.8984375
- gain_ffn: bfloat16 [960], P('dp'), may hold values from 0.099609375 to 1.8984375
- out_grad: bfloat16 [4096, 960], P(('dp', 'fsdp')), may hold values from -6 to 6
Outputs:
- block_out: bfloat16 [4096, 960], P(('dp', 'fsdp'))
- in_grad: float32 [4096, 960], P(('dp', 'fsdp'))
- grad_query: float32 [960, 960], P('dp', 'fsdp')
- grad_key: float32 [960, 320], P('dp', 'fsdp')
- grad_value: float32 [960, 320], P('dp', 'fsdp')
- grad_output: float32 [960, 960], P('dp', 'fsdp')
- grad_gate: float32 [960, 2560], P('dp', 'fsdp')
- grad_up: float32 [960, 2560], P('dp', 'fsdp')
- grad_down: float32 [2560, 960], P('dp', 'fsdp')
- grad_gain_attn: float32 [960], P('dp')
- grad_gain_ffn: float32 [960], P('dp')
The draws below stay inside these ranges and needn't reach their ends.
Inputs may be any that keep to these rules, and one draw needn't show every extreme that they name: `segment_ids`: along each row of 64 tokens the numbers never fall; each sequence holds at most 40 tokens.
All inputs are finite; a program needn't handle non-finite values.
Results may differ from the reference program's by a relative error of at most 0.015.
Values may be sent and summed in bfloat16 or wider, within the bound.
No kernel may reach another device: no remote copies, remote signals or barrier semaphores. Data moves between devices by JAX's collectives and lax.ppermute only.
A program may use at most 128 MiB of HBM per device.

```python
import math
import jax
import jax.numpy as jnp
import numpy as np
from jax import lax

D = 960
HEAD = 64
FF = 2560
MB_TOK = 64
SEGS = 3
SEQ_MOST = 40
KVD = 320
ROWS = 64
TOKENS = 4096


def spiked(entries, own_key, source, target, parts, factor):
    owner, partner = [(jnp.arange(entries.shape[position]) // (entries.shape[position] // parts)).reshape([-1 if axis == position else 1 for axis in range(entries.ndim)]) for position in (source, target)]
    chosen = jax.random.permutation(own_key, parts)[partner]
    strong = (owner == chosen) | (owner == (partner + parts // 2) % parts)
    return jnp.where(strong, factor * entries, entries)


def levels(rng, extent, shards, least, top_value):
    loudness = 1.0
    for axis_at, parts in shards:
        heights = jax.random.uniform(jax.random.fold_in(jax.random.fold_in(rng, 6), axis_at), (parts,), jnp.float32, least / len(shards), top_value / len(shards))
        loudness = loudness * jnp.repeat(jnp.exp(heights), extent[axis_at] // parts).reshape((-1,) + (1,) * (len(extent) - 1 - axis_at))
    return loudness


def split_up(number_of, total, reach, lean):
    weights = [(1 << 20) // math.isqrt(rank ** lean) + 1 for rank in range(2, number_of + 1)]
    spare, given = total - reach - (number_of - 1), [1] * (number_of - 1)
    while spare > 0:
        movable = [i for i in range(number_of - 1) if given[i] < reach]
        mass, remaining = sum([weights[i] for i in movable]), spare
        for i in movable:
            extra = min(reach - given[i], max(1, remaining * weights[i] // mass), spare)
            given[i] = given[i] + extra
            spare = spare - extra
    return np.array([reach] + given)


def ragged_sizes(own_key, amount, total, reach, skew):
    if amount == 2:
        one = jax.random.randint(own_key, (), max(1, total - reach), min(reach, total - 1) + 1)
        return jnp.stack([one, total - one])
    tallies = jnp.asarray(split_up(amount, total, reach, skew), jnp.int32)
    pairs = (amount - 1) // 2
    source_of, taker = tallies[1:1 + 2 * pairs:2], tallies[2:2 + 2 * pairs:2]
    margin = jnp.minimum(source_of - 1, reach - taker)
    moved = jax.random.randint(jax.random.fold_in(own_key, 1), (pairs,), 0, 1 << 20) % (margin + 1)
    tallies = tallies.at[1:1 + 2 * pairs:2].set(source_of - moved).at[2:2 + 2 * pairs:2].set(taker + moved)
    return tallies[jax.random.permutation(jax.random.fold_in(own_key, 2), amount)]


def normal_values(own_key, extent, width, most, split=(), kind=jnp.bfloat16):
    array = width * jax.random.normal(own_key, extent, jnp.float32)
    if split:
        array = array * levels(own_key, extent, split, -0.22, 0.18)
    return jnp.clip(array, -most, most).astype(kind)


def heavy_noise(own_key, extent, scale, reach, shards, heavy, kind=jnp.bfloat16):
    entries = scale * jax.random.normal(own_key, extent, jnp.float32)
    if shards:
        entries = entries * levels(own_key, extent, shards, -0.22, 0.18)
    return jnp.clip(spiked(entries, jax.random.fold_in(own_key, 3), *heavy), -reach, reach).astype(kind)


def setup_inputs(seed: int = 0) -> dict:
    key_list = jax.random.split(jax.random.key(seed), 13)
    tokens = heavy_noise(key_list[0], (TOKENS, D), 1.0, 6.0, ((0, 32),), (0, 1, 32, 2.75))
    segment_ids = jax.vmap(lambda own: jnp.searchsorted(jnp.cumsum(ragged_sizes(own, SEGS, MB_TOK, SEQ_MOST, 1)), jnp.arange(MB_TOK), side="right"))(jax.random.split(key_list[1], ROWS)).reshape((ROWS, MB_TOK)).astype(jnp.int32)
    w_query = normal_values(key_list[2], (D, D), D ** -0.5, 0.1875, ((0, 8), (1, 4)))
    w_key = normal_values(key_list[3], (D, KVD), D ** -0.5, 0.1875, ((0, 8), (1, 4)))
    w_value = normal_values(key_list[4], (D, KVD), D ** -0.5, 0.1875, ((0, 8), (1, 4)))
    w_output = normal_values(key_list[5], (D, D), (D // 16) ** -0.5, 0.75, ((0, 8), (1, 4)))
    w_gate = normal_values(key_list[6], (D, FF), D ** -0.5, 0.1875, ((0, 8), (1, 4)))
    w_up = normal_values(key_list[7], (D, FF), D ** -0.5, 0.1875, ((0, 8), (1, 4)))
    w_down = normal_values(key_list[8], (FF, D), FF ** -0.5, 0.125, ((0, 8), (1, 4)))
    gain_attn = jnp.clip(1.0 + 0.18 * jax.random.normal(key_list[9], (D,), jnp.float32), 0.099609375, 1.8984375).astype(jnp.bfloat16)
    gain_ffn = jnp.clip(1.0 + 0.18 * jax.random.normal(key_list[10], (D,), jnp.float32), 0.099609375, 1.8984375).astype(jnp.bfloat16)
    out_grad = heavy_noise(key_list[11], (TOKENS, D), 1.0, 6.0, ((0, 32),), (0, 1, 32, 2.75))
    return {"tokens": tokens, "segment_ids": segment_ids, "w_query": w_query, "w_key": w_key, "w_value": w_value, "w_output": w_output, "w_gate": w_gate, "w_up": w_up, "w_down": w_down, "gain_attn": gain_attn, "gain_ffn": gain_ffn, "out_grad": out_grad}


EPS = 1e-05
ROPE_BASE = 100000.0

def rope_tables(segment_row):
    length = segment_row.shape[0]
    token_index = jnp.arange(length, dtype=jnp.int32)
    change = jnp.concatenate([jnp.ones((1,), dtype=jnp.bool_), segment_row[1:] != segment_row[:-1]])
    starts = lax.cummax(jnp.where(change, token_index, 0).astype(jnp.int32), axis=0)
    offset = (token_index - starts).astype(jnp.float32)
    half_head = HEAD // 2
    frequency = ROPE_BASE ** (-jnp.arange(half_head, dtype=jnp.float32) / half_head)
    angles = offset[:, None] * frequency[None, :]
    return (jnp.cos(angles), jnp.sin(angles))

def allowed_pairs(segment_row):
    token_index = jnp.arange(segment_row.shape[0], dtype=jnp.int32)
    return (segment_row[:, None] == segment_row[None, :]) & (token_index[None, :] <= token_index[:, None])

def rotate(heads, cosine_table, sine_table):
    half_head = heads.shape[-1] // 2
    former = heads[..., :half_head]
    latter = heads[..., half_head:]
    cosine_wide = cosine_table[:, None, :]
    sine_wide = sine_table[:, None, :]
    return jnp.concatenate([former * cosine_wide - latter * sine_wide, latter * cosine_wide + former * sine_wide], axis=-1)

def unrotate(heads, cosine_table, sine_table):
    half_head = heads.shape[-1] // 2
    former = heads[..., :half_head]
    latter = heads[..., half_head:]
    cosine_wide = cosine_table[:, None, :]
    sine_wide = sine_table[:, None, :]
    return jnp.concatenate([former * cosine_wide + latter * sine_wide, latter * cosine_wide - former * sine_wide], axis=-1)

def product(form, left_side, right_side):
    return jnp.einsum(form, left_side.astype(jnp.float32), right_side.astype(jnp.float32), precision=lax.Precision.HIGHEST)

def times_transposed(left_side, right_side):
    return lax.dot_general(left_side, right_side, (((1,), (1,)), ((), ())), preferred_element_type=jnp.float32)

def outer_sum(left_side, right_side):
    return lax.dot_general(left_side, right_side, (((0,), (0,)), ((), ())), preferred_element_type=jnp.float32)

def forward_row(row_tokens, segment_row, weights):
    w_query, w_key, w_value, w_output, w_gate, w_up, w_down, gain_attn, gain_ffn = weights
    length = row_tokens.shape[0]
    query_heads = w_query.shape[1] // HEAD
    key_groups = w_key.shape[1] // HEAD
    group_size = query_heads // key_groups
    score_scale = HEAD ** (-0.5)
    cosine_table, sine_table = rope_tables(segment_row)
    allowed = allowed_pairs(segment_row)
    wide_tokens = row_tokens.astype(jnp.float32)
    inverse_attn = lax.rsqrt(lax.optimization_barrier(jnp.mean(wide_tokens * wide_tokens, axis=1, keepdims=True)) + EPS)
    normed_attn = (wide_tokens * inverse_attn * gain_attn.astype(jnp.float32)).astype(jnp.bfloat16)
    query_raw = jnp.dot(normed_attn, w_query, preferred_element_type=jnp.float32).reshape(length, query_heads, HEAD)
    query_rot = rotate(query_raw, cosine_table, sine_table).astype(jnp.bfloat16)
    key_raw = jnp.dot(normed_attn, w_key, preferred_element_type=jnp.float32).reshape(length, key_groups, HEAD)
    key_heads = rotate(key_raw, cosine_table, sine_table).astype(jnp.bfloat16)
    value_heads = jnp.dot(normed_attn, w_value, preferred_element_type=jnp.float32).astype(jnp.bfloat16).reshape(length, key_groups, HEAD)
    grouped = query_rot.reshape(length, key_groups, group_size, HEAD)
    scores = product('sgrd,tgd->grst', grouped, key_heads) * score_scale
    raised = jnp.where(allowed, jnp.exp(scores), 0.0)
    totals = lax.optimization_barrier(jnp.sum(raised, axis=-1, keepdims=True))
    log_total = jnp.log(totals)
    attn_probs = (raised / totals).astype(jnp.bfloat16)
    attn_in = product('grst,tgd->sgrd', attn_probs, value_heads).reshape(length, query_heads * HEAD).astype(jnp.bfloat16)
    middle = wide_tokens + jnp.dot(attn_in, w_output, preferred_element_type=jnp.float32)
    inverse_ffn = lax.rsqrt(lax.optimization_barrier(jnp.mean(middle * middle, axis=1, keepdims=True)) + EPS)
    normed_ffn = (middle * inverse_ffn * gain_ffn.astype(jnp.float32)).astype(jnp.bfloat16)
    gate_pre = jnp.dot(normed_ffn, w_gate, preferred_element_type=jnp.float32)
    upward = jnp.dot(normed_ffn, w_up, preferred_element_type=jnp.float32)
    hidden = (jax.nn.silu(gate_pre) * upward).astype(jnp.bfloat16)
    block_out = (middle + jnp.dot(hidden, w_down, preferred_element_type=jnp.float32)).astype(jnp.bfloat16)
    saved = (wide_tokens, inverse_attn, normed_attn, grouped, key_heads, value_heads, log_total, attn_in, middle, inverse_ffn, normed_ffn, gate_pre, upward, hidden)
    return (block_out, saved)

def backward_row(saved, segment_row, row_grad, weights):
    w_query, w_key, w_value, w_output, w_gate, w_up, w_down, gain_attn, gain_ffn = weights
    wide_tokens, inverse_attn, normed_attn, grouped, key_heads, value_heads, log_total, attn_in, middle, inverse_ffn, normed_ffn, gate_pre, upward, hidden = saved
    length = row_grad.shape[0]
    query_heads = w_query.shape[1] // HEAD
    key_groups = w_key.shape[1] // HEAD
    group_size = query_heads // key_groups
    score_scale = HEAD ** (-0.5)
    cosine_table, sine_table = rope_tables(segment_row)
    allowed = allowed_pairs(segment_row)
    wide_grad = row_grad.astype(jnp.float32)
    back_hidden = times_transposed(row_grad, w_down)
    sigmoid_gate = jax.nn.sigmoid(gate_pre)
    back_gate = (back_hidden * upward * sigmoid_gate * (1.0 + gate_pre * (1.0 - sigmoid_gate))).astype(jnp.bfloat16)
    back_upward = (back_hidden * gate_pre * sigmoid_gate).astype(jnp.bfloat16)
    back_normed_ffn = times_transposed(back_gate, w_gate) + times_transposed(back_upward, w_up)
    scaled_ffn = middle * inverse_ffn
    spread_ffn = back_normed_ffn * gain_ffn.astype(jnp.float32)
    gain_ffn_grad = lax.optimization_barrier(jnp.sum(back_normed_ffn * scaled_ffn, axis=0))
    back_middle = wide_grad + inverse_ffn * (spread_ffn - scaled_ffn * lax.optimization_barrier(jnp.mean(spread_ffn * scaled_ffn, axis=1, keepdims=True)))
    back_attn = back_middle.astype(jnp.bfloat16)
    back_heads = times_transposed(back_attn, w_output).astype(jnp.bfloat16).reshape(length, key_groups, group_size, HEAD)
    scores = product('sgrd,tgd->grst', grouped, key_heads) * score_scale
    probs_again = jnp.where(allowed, jnp.exp(scores - log_total), 0.0)
    probs_low = probs_again.astype(jnp.bfloat16)
    back_values = product('grst,sgrd->tgd', probs_low, back_heads).astype(jnp.bfloat16).reshape(length, key_groups * HEAD)
    back_probs = product('sgrd,tgd->grst', back_heads, value_heads)
    back_scores = (probs_again * (back_probs - lax.optimization_barrier(jnp.sum(probs_again * back_probs, axis=-1, keepdims=True)))).astype(jnp.bfloat16)
    query_back = (product('grst,tgd->sgrd', back_scores, key_heads) * score_scale).reshape(length, query_heads, HEAD)
    back_query = unrotate(query_back, cosine_table, sine_table).astype(jnp.bfloat16).reshape(length, query_heads * HEAD)
    key_back = product('grst,sgrd->tgd', back_scores, grouped) * score_scale
    back_keys = unrotate(key_back, cosine_table, sine_table).astype(jnp.bfloat16).reshape(length, key_groups * HEAD)
    back_normed_attn = times_transposed(back_query, w_query) + times_transposed(back_keys, w_key) + times_transposed(back_values, w_value)
    scaled_attn = wide_tokens * inverse_attn
    spread_attn = back_normed_attn * gain_attn.astype(jnp.float32)
    gain_attn_grad = lax.optimization_barrier(jnp.sum(back_normed_attn * scaled_attn, axis=0))
    in_grad = back_middle + inverse_attn * (spread_attn - scaled_attn * lax.optimization_barrier(jnp.mean(spread_attn * scaled_attn, axis=1, keepdims=True)))
    couples = ((normed_attn, back_query), (normed_attn, back_keys), (normed_attn, back_values), (attn_in, back_attn), (normed_ffn, back_gate), (normed_ffn, back_upward), (hidden, row_grad))
    return (in_grad, couples, gain_attn_grad, gain_ffn_grad)

def reference(tokens, segment_ids, w_query, w_key, w_value, w_output, w_gate, w_up, w_down, gain_attn, gain_ffn, out_grad):
    weights = (w_query, w_key, w_value, w_output, w_gate, w_up, w_down, gain_attn, gain_ffn)
    row_count = segment_ids.shape[0]
    length = segment_ids.shape[1]
    token_rows = tokens.reshape(row_count, length, tokens.shape[1])
    grad_rows = out_grad.reshape(row_count, length, out_grad.shape[1])

    def one_row(carry, inputs):
        row_tokens, segment_row, row_grad = inputs
        block_out, saved = forward_row(row_tokens, segment_row, weights)
        in_grad, couples, gain_attn_grad, gain_ffn_grad = backward_row(saved, segment_row, row_grad, weights)
        matrices = tuple((running + outer_sum(couple[0], couple[1]) for running, couple in zip(carry[:7], couples)))
        return (matrices + (carry[7] + gain_attn_grad, carry[8] + gain_ffn_grad), (block_out, in_grad))
    initial = tuple((jnp.zeros(weight.shape, jnp.float32) for weight in weights))
    carry, results = lax.scan(one_row, initial, (token_rows, segment_ids, grad_rows))
    block_out = results[0].reshape(tokens.shape)
    in_grad = results[1].reshape(tokens.shape)
    return (block_out, in_grad, carry[0], carry[1], carry[2], carry[3], carry[4], carry[5], carry[6], carry[7], carry[8])
```

```python
import jax
import jax.numpy as jnp
from jax import lax
from jax.sharding import PartitionSpec as P

HEAD = 64
EPS = 1e-05
ROPE_BASE = 100000.0
AXES = ("dp", "fsdp")
BF = jnp.bfloat16
F32 = jnp.float32


def mm(a, b):
    return lax.dot_general(a, b, (((1,), (0,)), ((), ())), preferred_element_type=F32)


def mm_t(a, b):
    return lax.dot_general(a, b, (((1,), (1,)), ((), ())), preferred_element_type=F32)


def t_mm(a, b):
    return lax.dot_general(a, b, (((0,), (0,)), ((), ())), preferred_element_type=F32)


def swap_blocks(blocks, amount):
    count = len(blocks)
    bit = 1
    while bit < count:
        chosen = (amount & bit) != 0
        blocks = [jnp.where(chosen, blocks[k ^ bit], blocks[k]) for k in range(count)]
        bit *= 2
    return blocks


class Plain:
    def __init__(self, mesh):
        self.parts = mesh.shape["fsdp"]
        self.halves = 1

    def gather(self, shard):
        rows = lax.all_gather(shard, "dp", axis=0, tiled=True)
        every = lax.all_gather(rows, "fsdp", axis=0, tiled=False)
        return {(f, 0): every[f] for f in range(self.parts)}

    def gather_gains(self, pair):
        return lax.all_gather(pair, "dp", axis=1, tiled=True)

    def reduce(self, make):
        stacked = jnp.stack([make(f, 0) for f in range(self.parts)])
        summed = lax.psum_scatter(stacked, "dp", scatter_dimension=1, tiled=True)
        return lax.psum_scatter(summed, "fsdp", scatter_dimension=0, tiled=False).astype(F32)

    def reduce_gains(self, pair):
        total = lax.psum(pair, AXES)
        width = pair.shape[1] // lax.axis_size("dp")
        return lax.dynamic_slice_in_dim(total, lax.axis_index("dp") * width, width, axis=1)

    def to_dp(self, x):
        return [x]

    def from_dp(self, parts):
        return parts[0]

    def to_f(self, x):
        return jnp.split(x, self.parts, axis=1)

    def from_f(self, blocks):
        return jnp.concatenate(blocks, axis=1)

    def order_f(self, blocks):
        return blocks

    def hidden_to_dp(self, blocks):
        return [jnp.concatenate(blocks, axis=1)]

    def hidden_from_dp(self, parts):
        return jnp.split(parts[0], self.parts, axis=1)


class Paired:
    def __init__(self, mesh):
        self.parts = mesh.shape["fsdp"]
        self.halves = 2
        self.deep = mesh.shape["dp"] // 2
        self.total = mesh.shape["dp"] * mesh.shape["fsdp"]
        self.f = lax.axis_index("fsdp")
        dp = lax.axis_index("dp")
        self.dp = dp
        self.y = dp % 2
        self.z = dp // 2

    def send(self, value, z=0, y=0, x=0, c=0):
        mask = ((z * 2 + y) * 2 + x) * 2 + c
        return lax.ppermute(value, AXES, [(i, i ^ mask) for i in range(self.total)])

    def gather(self, shard):
        own = jnp.concatenate(
            [shard] + [self.send(shard, z=k) for k in range(1, self.deep)], axis=0
        )
        half = own.shape[0] // 2
        side = self.send(own, x=1)
        over = self.send(own, y=1)
        across = jnp.concatenate(
            [self.send(side[:half], y=1), self.send(over[half:], x=1)], axis=0
        )
        pieces = {}
        for (kx, ky), piece in (((0, 0), own), ((1, 0), side), ((0, 1), over), ((1, 1), across)):
            pieces[(kx * 2, ky)] = piece
            pieces[(kx * 2 + 1, ky)] = self.send(piece, c=1)
        return pieces

    def gather_gains(self, pair):
        deep = jnp.stack([pair] + [self.send(pair, z=k) for k in range(1, self.deep)])
        both = jnp.stack([deep, self.send(deep, y=1)])
        flat = both.transpose(2, 0, 1, 3).reshape(2, -1)
        return mm_t(flat, self.dp_matrix(flat.shape[1])).astype(BF)

    def reduce(self, make):
        def joined(kx, ky):
            away = self.send(make(kx * 2 + 1, ky).astype(BF), c=1)
            return (make(kx * 2, ky) + away.astype(F32)).astype(BF)

        across = joined(1, 1)
        half = across.shape[0] // 2
        to_side = self.send(across[:half], y=1)
        to_over = self.send(across[half:], x=1)
        side = joined(1, 0)
        side = jnp.concatenate(
            [(side[:half].astype(F32) + to_side.astype(F32)).astype(BF), side[half:]], axis=0
        )
        from_side = self.send(side, x=1)
        over = joined(0, 1)
        over = jnp.concatenate(
            [over[:half], (over[half:].astype(F32) + to_over.astype(F32)).astype(BF)], axis=0
        )
        from_over = self.send(over, y=1)
        own = joined(0, 0).astype(F32) + from_side.astype(F32) + from_over.astype(F32)
        rows = own.shape[0] // self.deep
        result = own[:rows]
        for k in range(1, self.deep):
            part = own[k * rows : (k + 1) * rows].astype(BF)
            result = result + self.send(part, z=k).astype(F32)
        return result

    def reduce_gains(self, pair):
        total = pair + self.send(pair, c=1)
        total = total + self.send(total, x=1)
        total = total + self.send(total, y=1)
        total = total + sum(self.send(total, z=k) for k in range(1, self.deep))
        width = pair.shape[1] // (2 * self.deep)
        return lax.dynamic_slice_in_dim(total, self.dp * width, width, axis=1)

    def dp_matrix(self, extent):
        width = extent // (2 * self.deep)
        place = jnp.arange(extent, dtype=jnp.int32)
        block, within = place // width, place % width
        ky, kz = block // self.deep, block % self.deep
        source = ((self.z ^ kz) * 2 + (self.y ^ ky)) * width + within
        return (jnp.arange(extent, dtype=jnp.int32)[:, None] == source[None, :]).astype(BF)

    def f_matrix(self, extent):
        width = extent // self.parts
        place = jnp.arange(extent, dtype=jnp.int32)
        source = (self.f ^ (place // width)) * width + place % width
        return (jnp.arange(extent, dtype=jnp.int32)[:, None] == source[None, :]).astype(BF)

    def to_dp(self, x):
        turned = mm(x, self.dp_matrix(x.shape[1])).astype(BF)
        return jnp.split(turned, 2, axis=1)

    def from_dp(self, parts):
        whole = jnp.concatenate(parts, axis=1)
        matrix = self.dp_matrix(whole.shape[1]).astype(F32)
        return lax.dot_general(
            whole, matrix, (((1,), (1,)), ((), ())), precision=lax.Precision.HIGH
        )

    def to_f(self, x):
        turned = mm(x, self.f_matrix(x.shape[1])).astype(BF)
        return jnp.split(turned, self.parts, axis=1)

    def from_f(self, blocks):
        return jnp.concatenate(swap_blocks(blocks, self.f), axis=1)

    def order_f(self, blocks):
        return swap_blocks(blocks, self.f)

    def hidden_to_dp(self, blocks):
        blocks = swap_blocks(blocks, self.z ^ self.f)
        half = blocks[0].shape[1] // 2
        low = [b[:, :half] for b in blocks]
        high = [b[:, half:] for b in blocks]
        odd = self.y == 1
        near = [jnp.where(odd, h, l) for l, h in zip(low, high)]
        far = [jnp.where(odd, l, h) for l, h in zip(low, high)]
        return [jnp.concatenate(near, axis=1), jnp.concatenate(far, axis=1)]

    def hidden_from_dp(self, parts):
        near = jnp.split(parts[0], self.deep, axis=1)
        far = jnp.split(parts[1], self.deep, axis=1)
        odd = self.y == 1
        blocks = [
            jnp.concatenate([jnp.where(odd, b, a), jnp.where(odd, a, b)], axis=1)
            for a, b in zip(near, far)
        ]
        return swap_blocks(blocks, self.z ^ self.f)


def make_plan(mesh):
    dp, parts = mesh.shape["dp"], mesh.shape["fsdp"]
    if parts == 4 and dp == 2 * parts:
        return Paired(mesh)
    return Plain(mesh)


def rotate(heads, cosine, sine):
    half = heads.shape[-1] // 2
    u, w = heads[..., :half], heads[..., half:]
    return jnp.concatenate([u * cosine - w * sine, w * cosine + u * sine], axis=-1)


def unrotate(heads, cosine, sine):
    half = heads.shape[-1] // 2
    u, w = heads[..., :half], heads[..., half:]
    return jnp.concatenate([u * cosine + w * sine, w * cosine - u * sine], axis=-1)


def product(form, a, b):
    return jnp.einsum(form, a, b, preferred_element_type=F32)


def on_device(mesh, tokens, segment_ids, w_query, w_key, w_value, w_output, w_gate, w_up, w_down,
              gain_attn, gain_ffn, out_grad):
    plan = make_plan(mesh)
    parts, halves = plan.parts, plan.halves
    rows, length = segment_ids.shape
    count, width = tokens.shape
    q_cols, k_cols, o_cols = w_query.shape[1], w_key.shape[1], w_output.shape[1]
    heads = q_cols * parts // HEAD
    groups = k_cols * parts // HEAD
    per_group = heads // groups
    score_scale = HEAD ** (-0.5)

    gains = plan.gather_gains(jnp.stack([gain_attn, gain_ffn]))
    attn = plan.gather(jnp.concatenate([w_output, w_query, w_key, w_value], axis=1))
    down = plan.gather(w_down)
    gate_w = plan.gather(w_gate)
    up_w = plan.gather(w_up)
    gain_a = gains[0:1].astype(F32)
    gain_f = gains[1:2].astype(F32)

    same = segment_ids[:, :, None] == segment_ids[:, None, :]
    before = segment_ids[:, None, :] < segment_ids[:, :, None]
    index = jnp.arange(length, dtype=jnp.int32)
    pos = (index[None, :] - jnp.sum(before.astype(jnp.int32), axis=-1)).astype(F32)
    half_head = HEAD // 2
    frequency = ROPE_BASE ** (-jnp.arange(half_head, dtype=F32) / half_head)
    angles = pos[:, :, None, None] * frequency
    cosine, sine = jnp.cos(angles), jnp.sin(angles)
    allowed = (same & (index[None, :] <= index[:, None])[None])[:, None, None]

    wide = tokens.astype(F32)
    inv1 = lax.rsqrt(jnp.mean(wide * wide, axis=1, keepdims=True) + EPS)
    normed1 = (wide * inv1 * gain_a).astype(BF)
    normed1_dp = plan.to_dp(normed1)
    mixed = plan.order_f(
        [sum(mm(normed1_dp[y], attn[(f, y)]) for y in range(halves)) for f in range(parts)]
    )
    at = o_cols
    query = jnp.concatenate([m[:, at : at + q_cols] for m in mixed], axis=1)
    at += q_cols
    key = jnp.concatenate([m[:, at : at + k_cols] for m in mixed], axis=1)
    at += k_cols
    value = jnp.concatenate([m[:, at:] for m in mixed], axis=1).astype(BF)
    query = rotate(query.reshape(rows, length, heads, HEAD), cosine, sine).astype(BF)
    query = query.reshape(rows, length, groups, per_group, HEAD)
    key = rotate(key.reshape(rows, length, groups, HEAD), cosine, sine).astype(BF)
    value = value.reshape(rows, length, groups, HEAD)
    scores = product("bsgrd,btgd->bgrst", query, key) * score_scale
    raised = jnp.where(allowed, jnp.exp(scores), 0.0)
    probs = raised / jnp.sum(raised, axis=-1, keepdims=True)
    probs_low = probs.astype(BF)
    attn_in = product("bgrst,btgd->bsgrd", probs_low, value).reshape(count, width).astype(BF)
    attn_in_dp = plan.to_dp(attn_in)
    projected = [
        sum(mm(attn_in_dp[y], attn[(f, y)][:, :o_cols]) for y in range(halves))
        for f in range(parts)
    ]
    mid = wide + plan.from_f(projected)

    inv2 = lax.rsqrt(jnp.mean(mid * mid, axis=1, keepdims=True) + EPS)
    scaled2 = mid * inv2
    normed2 = (scaled2 * gain_f).astype(BF)
    normed2_dp = plan.to_dp(normed2)
    og_f = plan.to_f(out_grad)
    d_act = plan.hidden_from_dp(
        [sum(mm_t(og_f[f], down[(f, y)]) for f in range(parts)) for y in range(halves)]
    )
    acts, d_gate, d_up = [], [], []
    for f in range(parts):
        gate = sum(mm(normed2_dp[y], gate_w[(f, y)]) for y in range(halves))
        upward = sum(mm(normed2_dp[y], up_w[(f, y)]) for y in range(halves))
        sg = jax.nn.sigmoid(gate)
        silu = gate * sg
        acts.append((silu * upward).astype(BF))
        d_gate.append((d_act[f] * upward * sg * (1.0 + gate * (1.0 - sg))).astype(BF))
        d_up.append((d_act[f] * silu).astype(BF))
    act_dp = plan.hidden_to_dp(acts)

    grad_gate = plan.reduce(lambda f, y: t_mm(normed2_dp[y], d_gate[f]))
    grad_up = plan.reduce(lambda f, y: t_mm(normed2_dp[y], d_up[f]))
    grad_down = plan.reduce(lambda f, y: t_mm(act_dp[y], og_f[f]))

    d_normed2 = plan.from_dp(
        [
            sum(mm_t(d_gate[f], gate_w[(f, y)]) + mm_t(d_up[f], up_w[(f, y)]) for f in range(parts))
            for y in range(halves)
        ]
    )
    e2 = d_normed2 * gain_f
    d_mid = out_grad.astype(F32) + inv2 * (
        e2 - scaled2 * jnp.mean(e2 * scaled2, axis=1, keepdims=True)
    )
    d_attn = d_mid.astype(BF)
    d_attn_f = plan.to_f(d_attn)

    d_heads_dp = [
        sum(mm_t(d_attn_f[f], attn[(f, y)][:, :o_cols]) for f in range(parts)).astype(F32)
        for y in range(halves)
    ]
    d_heads = plan.from_dp(d_heads_dp).astype(BF).reshape(rows, length, groups, per_group, HEAD)
    d_value = product("bgrst,bsgrd->btgd", probs_low, d_heads).astype(BF)
    d_probs = product("bsgrd,btgd->bgrst", d_heads, value)
    d_scores = (
        probs * (d_probs - jnp.sum(probs * d_probs, axis=-1, keepdims=True))
    ).astype(BF)
    d_query = product("bgrst,btgd->bsgrd", d_scores, key) * score_scale
    d_query = unrotate(d_query.reshape(rows, length, heads, HEAD), cosine, sine)
    d_query = d_query.astype(BF).reshape(count, heads * HEAD)
    d_key = product("bgrst,bsgrd->btgd", d_scores, query) * score_scale
    d_key = unrotate(d_key, cosine, sine).astype(BF).reshape(count, groups * HEAD)
    d_value = d_value.reshape(count, groups * HEAD)
    blank = jnp.zeros((count, o_cols), BF)
    d_mixed = plan.order_f(
        [
            jnp.concatenate(
                [
                    blank,
                    d_query[:, f * q_cols : (f + 1) * q_cols],
                    d_key[:, f * k_cols : (f + 1) * k_cols],
                    d_value[:, f * k_cols : (f + 1) * k_cols],
                ],
                axis=1,
            )
            for f in range(parts)
        ]
    )
    rest = jnp.zeros((count, q_cols + 2 * k_cols), BF)
    tall = [jnp.concatenate([a, b], axis=0) for a, b in zip(attn_in_dp, normed1_dp)]
    flat = [
        jnp.concatenate([jnp.concatenate([d_attn_f[f], rest], axis=1), d_mixed[f]], axis=0)
        for f in range(parts)
    ]
    grad_attn = plan.reduce(lambda f, y: t_mm(tall[y], flat[f]))
    d_normed1 = plan.from_dp(
        [sum(mm_t(d_mixed[f], attn[(f, y)]) for f in range(parts)) for y in range(halves)]
    )
    scaled1 = wide * inv1
    e1 = d_normed1 * gain_a
    in_grad = d_mid + inv1 * (e1 - scaled1 * jnp.mean(e1 * scaled1, axis=1, keepdims=True))
    grad_gains = plan.reduce_gains(
        jnp.stack([jnp.sum(d_normed1 * scaled1, axis=0), jnp.sum(d_normed2 * scaled2, axis=0)])
    )

    lifted = [
        sum(mm(act_dp[y], down[(f, y)]) for y in range(halves)) for f in range(parts)
    ]
    block_out = (mid + plan.from_f(lifted)).astype(BF)

    a, b, c = o_cols, o_cols + q_cols, o_cols + q_cols + k_cols
    return (
        block_out,
        in_grad,
        grad_attn[:, a:b],
        grad_attn[:, b:c],
        grad_attn[:, c:],
        grad_attn[:, :a],
        grad_gate,
        grad_up,
        grad_down,
        grad_gains[0],
        grad_gains[1],
    )


def solution(mesh):
    token = P(AXES, None)
    matrix = P("dp", "fsdp")
    gain = P("dp")

    def body(*args):
        return on_device(mesh, *args)

    return jax.shard_map(
        body,
        mesh=mesh,
        in_specs=(token, token) + (matrix,) * 7 + (gain, gain, token),
        out_specs=(token, token) + (matrix,) * 7 + (gain, gain),
        check_vma=False,
    )
```

```python
import jax
import jax.numpy as jnp
from jax import lax
from jax.experimental import pallas as pl
from jax.experimental.pallas import tpu as pltpu
from jax.sharding import PartitionSpec as P

HEAD = 64
EPS = 1e-05
ROPE_BASE = 100000.0
AXES = ("dp", "fsdp")
BF = jnp.bfloat16
F32 = jnp.float32


def mm(a, b):
    return lax.dot_general(a, b, (((1,), (0,)), ((), ())), preferred_element_type=F32)


def mm_t(a, b):
    return lax.dot_general(a, b, (((1,), (1,)), ((), ())), preferred_element_type=F32)


def t_mm(a, b):
    return lax.dot_general(a, b, (((0,), (0,)), ((), ())), preferred_element_type=F32)


def swap_blocks(blocks, amount):
    count = len(blocks)
    bit = 1
    while bit < count:
        chosen = (amount & bit) != 0
        blocks = [jnp.where(chosen, blocks[k ^ bit], blocks[k]) for k in range(count)]
        bit *= 2
    return blocks


def tie(value, *others):
    return lax.optimization_barrier((value,) + others)[0]


VMEM_BYTES = 60000 * 1024


def pieces_away(make, operands, shape, places):
    def kernel(*refs):
        out = refs[-1]
        for n, (kx, ky) in enumerate(places):
            for h in range(2):
                out[n, h] = make(refs[:-1], kx * 2 + 1, ky, h).astype(BF)

    return pl.pallas_call(
        kernel,
        out_shape=jax.ShapeDtypeStruct((len(places),) + shape, BF),
        compiler_params=pltpu.CompilerParams(vmem_limit_bytes=VMEM_BYTES),
        name="pieces_away",
    )(*operands)


def pieces_joined(make, operands, shape, places, received):
    def kernel(*refs):
        count = len(operands)
        got, outs = refs[count], refs[count + 1 :]
        for n, (kx, ky) in enumerate(places):
            for h in range(2):
                mine = make(refs[:count], kx * 2, ky, h)
                outs[n][h] = (mine + got[n, h].astype(F32)).astype(BF)

    return pl.pallas_call(
        kernel,
        out_shape=[jax.ShapeDtypeStruct(shape, BF) for _ in places],
        compiler_params=pltpu.CompilerParams(vmem_limit_bytes=VMEM_BYTES),
        name="pieces_joined",
    )(*operands, received)


def halves_of(x):
    high = x.astype(BF)
    return high, (x - high.astype(F32)).astype(BF)


def select_back(x, matrix):
    high, low = halves_of(x)
    return mm_t(high, matrix) + mm_t(low, matrix)


def kernel_call(kernel, name, operands, in_specs, out_shape, scratch_shapes=()):
    vmem = pl.BlockSpec(memory_space=pltpu.VMEM)
    return pl.pallas_call(
        kernel,
        in_specs=in_specs,
        out_specs=[vmem] * len(out_shape),
        out_shape=out_shape,
        scratch_shapes=list(scratch_shapes),
        compiler_params=pltpu.CompilerParams(vmem_limit_bytes=VMEM_BYTES),
        name=name,
    )(*operands)


def specs(smem, vmem, anywhere=0):
    return (
        [pl.BlockSpec(memory_space=pltpu.SMEM)] * smem
        + [pl.BlockSpec(memory_space=pltpu.VMEM)] * vmem
        + [pl.BlockSpec(memory_space=pl.ANY)] * anywhere
    )


def feed_forward(place, normed_q, og_f, mid, down, gate_up):
    parts, count, _ = og_f.shape
    deep = parts
    rows = gate_up[0].shape[1]
    hidden = gate_up[0].shape[2]
    half = hidden // 2
    cut = rows // 2
    pairs = len(down)

    def kernel(place_ref, n_ref, og_ref, mid_ref, *refs):
        down_hbm, gu_hbm = refs[:pairs], refs[pairs : 2 * pairs]
        act_ref, dg_ref, du_ref, dn_ref, out_ref = refs[2 * pairs : 2 * pairs + 5]
        down_v, gu_v, turn_ref, back_ref, lift_ref, down_sem, gu_sem = refs[2 * pairs + 5 :]
        down_copies = [
            pltpu.make_async_copy(down_hbm[i], down_v.at[i], down_sem.at[i]) for i in range(pairs)
        ]
        gu_copies = [
            pltpu.make_async_copy(gu_hbm[i], gu_v.at[i], gu_sem.at[i]) for i in range(pairs)
        ]
        for copy in down_copies + gu_copies:
            copy.start()
        turn, odd, me = place_ref[0], place_ref[1], place_ref[2]
        for copy in down_copies:
            copy.wait()
        for ky in range(2):
            for h in range(2):
                total = mm(og_ref[0], down_v[ky, h])
                for f in range(1, parts):
                    total = total + mm(og_ref[f], down_v[f * 2 + ky, h])
                turn_ref[ky, 2 * h] = total[:, :half]
                turn_ref[ky, 2 * h + 1] = total[:, half:]
        for kz in range(deep):
            back_ref[kz ^ turn] = jnp.concatenate(
                [turn_ref[odd, kz], turn_ref[1 - odd, kz]], axis=1
            )

        def product(i, h):
            return mm(n_ref[0], gu_v[2 * i, h, :cut]) + mm(n_ref[1], gu_v[2 * i, h, cut:]) + (
                mm(n_ref[2], gu_v[2 * i + 1, h, :cut]) + mm(n_ref[3], gu_v[2 * i + 1, h, cut:])
            )

        for f in range(parts):
            gu_copies[2 * f].wait()
            gu_copies[2 * f + 1].wait()
            gate, upward = product(f, 0), product(f, 1)
            sg = jax.nn.sigmoid(gate)
            silu = gate * sg
            act = silu * upward
            turn_ref[odd, f ^ turn] = act[:, :half]
            turn_ref[1 - odd, f ^ turn] = act[:, half:]
            back = back_ref[f]
            dg_ref[f] = (back * upward * sg * (1.0 + gate * (1.0 - sg))).astype(BF)
            du_ref[f] = (back * silu).astype(BF)
        for ky in range(2):
            for h in range(2):
                act_ref[ky, h] = jnp.concatenate(
                    [turn_ref[ky, 2 * h], turn_ref[ky, 2 * h + 1]], axis=1
                ).astype(BF)
            for h in range(2):
                total = None
                for f in range(parts):
                    spot = pl.ds(h * cut, cut)
                    here = mm_t(dg_ref[f], gu_v[2 * f + ky, 0, spot]) + mm_t(
                        du_ref[f], gu_v[2 * f + ky, 1, spot]
                    )
                    total = here if total is None else total + here
                dn_ref[2 * ky + h] = total
        for f in range(parts):
            total = None
            for ky in range(2):
                for h in range(2):
                    here = mm_t(act_ref[ky, h], down_v[f * 2 + ky, h])
                    total = here if total is None else total + here
            lift_ref[f ^ me] = total
        lifted = jnp.concatenate([lift_ref[f] for f in range(parts)], axis=1)
        out_ref[...] = (mid_ref[...] + lifted).astype(BF)

    return kernel_call(
        kernel,
        "feed_forward",
        (place, normed_q, og_f, mid, *down, *gate_up),
        specs(1, 3, 2 * pairs),
        [
            jax.ShapeDtypeStruct((2, 2, count, hidden), BF),
            jax.ShapeDtypeStruct((parts, count, hidden), BF),
            jax.ShapeDtypeStruct((parts, count, hidden), BF),
            jax.ShapeDtypeStruct(normed_q.shape, F32),
            jax.ShapeDtypeStruct(mid.shape, BF),
        ],
        [
            pltpu.VMEM((pairs,) + down[0].shape, BF),
            pltpu.VMEM((pairs,) + gate_up[0].shape, BF),
            pltpu.VMEM((2, deep, count, half), F32),
            pltpu.VMEM((parts, count, hidden), F32),
            pltpu.VMEM(og_f.shape, F32),
            pltpu.SemaphoreType.DMA((pairs,)),
            pltpu.SemaphoreType.DMA((pairs,)),
        ],
    )


def partner(x):
    half = x.shape[1] // 2
    return jnp.concatenate([x[:, half:], x[:, :half]], axis=1)


def attention_forward(place, tokens, gains, cosine, sine, allowed, to_dp, pieces, sizes):
    o_cols, q_cols, k_cols = sizes
    count, width = tokens.shape
    parts = len(pieces) // 2
    heads, groups = parts * q_cols // HEAD, parts * k_cols // HEAD
    per_group = heads // groups
    scale = HEAD ** (-0.5)
    quarter = to_dp.shape[2]

    def kernel(place_ref, x_ref, gain_ref, cos_ref, sin_ref, ok_ref, dp_ref, *refs):
        w, outs = refs[: 2 * parts], refs[2 * parts :]
        tall_ref, mid_ref, n2_ref, p_ref, q_ref, k_ref, v_ref, mix_ref, lift_ref = outs
        me = place_ref[2]
        wide = x_ref[...].astype(F32)
        inverse = lax.rsqrt(jnp.mean(wide * wide, axis=1, keepdims=True) + EPS)
        normed = (wide * inverse * gain_ref[0:1].astype(F32)).astype(BF)
        for i in range(4):
            tall_ref[i, count:] = mm(normed, dp_ref[i]).astype(BF)
        for f in range(parts):
            total = None
            for i in range(4):
                here = mm(tall_ref[i, count:], w[2 * f + i // 2][i % 2])
                total = here if total is None else total + here
            mix_ref[f ^ me] = total
        at = o_cols
        query = jnp.concatenate([mix_ref[f][:, at : at + q_cols] for f in range(parts)], axis=1)
        at += q_cols
        key = jnp.concatenate([mix_ref[f][:, at : at + k_cols] for f in range(parts)], axis=1)
        at += k_cols
        value = jnp.concatenate([mix_ref[f][:, at:] for f in range(parts)], axis=1)
        cos, sin = cos_ref[...], sin_ref[...]

        def turned(all_heads, h):
            x = all_heads[:, h * HEAD : (h + 1) * HEAD]
            return (x * cos + partner(x) * sin).astype(BF)

        allow = jnp.concatenate([ok_ref[...]] * per_group, axis=0) != 0.0
        done = []
        for g in range(groups):
            k = turned(key, g)
            v = value[:, g * HEAD : (g + 1) * HEAD].astype(BF)
            q = jnp.concatenate([turned(query, g * per_group + j) for j in range(per_group)], axis=0)
            q_ref[g], k_ref[g], v_ref[g] = q, k, v
            scores = mm_t(q, k) * scale
            raised = jnp.where(allow, jnp.exp(scores), 0.0)
            probs = raised / jnp.sum(raised, axis=1, keepdims=True)
            p_ref[g] = probs
            got = mm(probs.astype(BF), v)
            done += [got[j * count : (j + 1) * count] for j in range(per_group)]
        attn_in = jnp.concatenate(done, axis=1).astype(BF)
        for i in range(4):
            tall_ref[i, :count] = mm(attn_in, dp_ref[i]).astype(BF)
        for f in range(parts):
            total = None
            for i in range(4):
                here = mm(tall_ref[i, :count], w[2 * f + i // 2][i % 2][:, :o_cols])
                total = here if total is None else total + here
            lift_ref[f ^ me] = total
        mid = wide + jnp.concatenate([lift_ref[f] for f in range(parts)], axis=1)
        mid_ref[...] = mid
        inverse = lax.rsqrt(jnp.mean(mid * mid, axis=1, keepdims=True) + EPS)
        normed = (mid * inverse * gain_ref[1:2].astype(F32)).astype(BF)
        for i in range(4):
            n2_ref[i] = mm(normed, dp_ref[i]).astype(BF)

    return kernel_call(
        kernel,
        "attention_forward",
        (place, tokens, gains, cosine, sine, allowed, to_dp, *pieces),
        specs(1, 6 + 2 * parts),
        [
            jax.ShapeDtypeStruct((4, 2 * count, quarter), BF),
            jax.ShapeDtypeStruct((count, width), F32),
            jax.ShapeDtypeStruct((4, count, quarter), BF),
            jax.ShapeDtypeStruct((groups, per_group * count, count), F32),
            jax.ShapeDtypeStruct((groups, per_group * count, HEAD), BF),
            jax.ShapeDtypeStruct((groups, count, HEAD), BF),
            jax.ShapeDtypeStruct((groups, count, HEAD), BF),
        ],
        [
            pltpu.VMEM((parts, count, o_cols + q_cols + 2 * k_cols), F32),
            pltpu.VMEM((parts, count, o_cols), F32),
        ],
    )


def attention_backward(place, tokens, gains, cosine, sine, to_dp, to_f, out_grad, mid,
                       d_normed_q, kept, pieces, sizes):
    o_cols, q_cols, k_cols = sizes
    count, width = tokens.shape
    parts = len(pieces) // 2
    heads, groups = parts * q_cols // HEAD, parts * k_cols // HEAD
    per_group = heads // groups
    scale = HEAD ** (-0.5)
    every = o_cols + q_cols + 2 * k_cols

    def kernel(place_ref, x_ref, gain_ref, cos_ref, sin_ref, dp_ref, f_ref, og_ref, mid_ref,
               dn_ref, p_ref, q_ref, k_ref, v_ref, *refs):
        w, outs = refs[: 2 * parts], refs[2 * parts :]
        flat_ref, grad_ref, gains_ref = outs
        me = place_ref[2]
        gain_a = gain_ref[0:1].astype(F32)
        gain_f = gain_ref[1:2].astype(F32)

        def gathered(blocks):
            total = None
            for i in range(4):
                here = select_back(blocks[i], dp_ref[i])
                total = here if total is None else total + here
            return total

        mid = mid_ref[...]
        inverse = lax.rsqrt(jnp.mean(mid * mid, axis=1, keepdims=True) + EPS)
        scaled = mid * inverse
        d_normed = gathered([dn_ref[i] for i in range(4)])
        gains_ref[1:2] = jnp.sum(d_normed * scaled, axis=0, keepdims=True)
        spread = d_normed * gain_f
        d_mid = og_ref[...].astype(F32) + inverse * (
            spread - scaled * jnp.mean(spread * scaled, axis=1, keepdims=True)
        )
        d_attn = d_mid.astype(BF)
        for f in range(parts):
            block = mm(d_attn, f_ref[f])
            flat_ref[f, :count] = jnp.concatenate(
                [block, jnp.zeros((count, every - o_cols), F32)], axis=1
            ).astype(BF)
        d_heads = None
        for i in range(4):
            total = None
            for f in range(parts):
                here = mm_t(
                    flat_ref[f, :count][:, :o_cols], w[2 * f + i // 2][i % 2][:, :o_cols]
                )
                total = here if total is None else total + here
            here = mm_t(total.astype(BF), dp_ref[i])
            d_heads = here if d_heads is None else d_heads + here
        cos, sin = cos_ref[...], sin_ref[...]

        def unturned(x):
            return (x * cos - partner(x) * sin).astype(BF).astype(F32)

        d_query, d_key, d_value = [], [], []
        for g in range(groups):
            first = g * per_group
            dh = jnp.concatenate(
                [d_heads[:, (first + j) * HEAD : (first + j + 1) * HEAD] for j in range(per_group)],
                axis=0,
            ).astype(BF)
            q, k, v, probs = q_ref[g], k_ref[g], v_ref[g], p_ref[g]
            d_value.append(t_mm(probs.astype(BF), dh).astype(BF).astype(F32))
            d_probs = mm_t(dh, v)
            ds = (
                probs * (d_probs - jnp.sum(probs * d_probs, axis=1, keepdims=True))
            ).astype(BF)
            dq = mm(ds, k) * scale
            d_query += [unturned(dq[j * count : (j + 1) * count]) for j in range(per_group)]
            d_key.append(unturned(t_mm(ds, q) * scale))
        d_query = jnp.concatenate(d_query, axis=1)
        d_key = jnp.concatenate(d_key, axis=1)
        d_value = jnp.concatenate(d_value, axis=1)
        for f in range(parts):
            flat_ref[f ^ me, count:] = jnp.concatenate(
                [
                    jnp.zeros((count, o_cols), F32),
                    d_query[:, f * q_cols : (f + 1) * q_cols],
                    d_key[:, f * k_cols : (f + 1) * k_cols],
                    d_value[:, f * k_cols : (f + 1) * k_cols],
                ],
                axis=1,
            ).astype(BF)
        blocks = []
        for i in range(4):
            total = None
            for f in range(parts):
                here = mm_t(flat_ref[f, count:], w[2 * f + i // 2][i % 2])
                total = here if total is None else total + here
            blocks.append(total)
        d_normed = gathered(blocks)
        wide = x_ref[...].astype(F32)
        inverse = lax.rsqrt(jnp.mean(wide * wide, axis=1, keepdims=True) + EPS)
        scaled = wide * inverse
        gains_ref[0:1] = jnp.sum(d_normed * scaled, axis=0, keepdims=True)
        spread = d_normed * gain_a
        grad_ref[...] = d_mid + inverse * (
            spread - scaled * jnp.mean(spread * scaled, axis=1, keepdims=True)
        )

    return kernel_call(
        kernel,
        "attention_backward",
        (place, tokens, gains, cosine, sine, to_dp, to_f, out_grad, mid, d_normed_q,
         *kept, *pieces),
        specs(1, 13 + 2 * parts),
        [
            jax.ShapeDtypeStruct((parts, 2 * count, every), BF),
            jax.ShapeDtypeStruct((count, width), F32),
            jax.ShapeDtypeStruct((2, width), F32),
        ],
    )


class Plain:
    def __init__(self, mesh):
        self.parts = mesh.shape["fsdp"]
        self.halves = 1

    def gather(self, shard):
        rows = lax.all_gather(shard, "dp", axis=0, tiled=True)
        every = lax.all_gather(rows, "fsdp", axis=0, tiled=False)
        return {(f, 0): every[f] for f in range(self.parts)}

    def gather_gains(self, pair):
        return lax.all_gather(pair, "dp", axis=1, tiled=True)

    def reduce(self, make):
        stacked = jnp.stack([make(f, 0) for f in range(self.parts)])
        summed = lax.psum_scatter(stacked, "dp", scatter_dimension=1, tiled=True)
        return lax.psum_scatter(summed, "fsdp", scatter_dimension=0, tiled=False).astype(F32)

    def reduce_gains(self, pair):
        total = lax.psum(pair, AXES)
        width = pair.shape[1] // lax.axis_size("dp")
        return lax.dynamic_slice_in_dim(total, lax.axis_index("dp") * width, width, axis=1)

    def to_dp(self, x):
        return [x]

    def from_dp(self, parts):
        return parts[0]

    def to_f(self, x):
        return jnp.split(x, self.parts, axis=1)

    def from_f(self, blocks):
        return jnp.concatenate(blocks, axis=1)

    def order_f(self, blocks):
        return blocks

    def hidden_to_dp(self, blocks):
        return [jnp.concatenate(blocks, axis=1)]

    def hidden_from_dp(self, parts):
        return jnp.split(parts[0], self.parts, axis=1)


class Paired:
    def __init__(self, mesh):
        self.parts = mesh.shape["fsdp"]
        self.halves = 2
        self.deep = mesh.shape["dp"] // 2
        self.total = mesh.shape["dp"] * mesh.shape["fsdp"]
        self.f = lax.axis_index("fsdp")
        dp = lax.axis_index("dp")
        self.dp = dp
        self.y = dp % 2
        self.z = dp // 2

    def send(self, value, z=0, y=0, x=0, c=0):
        mask = ((z * 2 + y) * 2 + x) * 2 + c
        return lax.ppermute(value, AXES, [(i, i ^ mask) for i in range(self.total)])

    def spread(self, shard):
        axis = shard.ndim - 2
        own = jnp.concatenate(
            [shard] + [self.send(shard, z=k) for k in range(1, self.deep)], axis=axis
        )
        return own if own.ndim == 3 else own.reshape(2, -1, own.shape[1])

    def widen(self, own):
        return self.send(own, x=1), self.send(own, y=1)

    def cross(self, side, over):
        return jnp.stack([self.send(side[0], y=1), self.send(over[1], x=1)])

    def complete(self, own, side, over, across):
        pieces = {}
        for (kx, ky), piece in (((0, 0), own), ((1, 0), side), ((0, 1), over), ((1, 1), across)):
            pieces[(kx * 2, ky)] = piece
            pieces[(kx * 2 + 1, ky)] = self.send(piece, c=1)
        return pieces

    def gather_gains(self, pair):
        deep = jnp.stack([pair] + [self.send(pair, z=k) for k in range(1, self.deep)])
        both = jnp.stack([deep, self.send(deep, y=1)])
        flat = both.transpose(2, 0, 1, 3).reshape(2, -1)
        return mm_t(flat, self.dp_matrix(flat.shape[1])).astype(BF)

    def start(self, make, operands, shape):
        first, rest = ((1, 1),), ((1, 0), (0, 1), (0, 0))
        away_first = self.send(pieces_away(make, operands, shape, first), c=1)
        away_rest = self.send(pieces_away(make, operands, shape, rest), c=1)
        return make, operands, shape, first, rest, away_first, away_rest

    def join(self, begun):
        make, operands, shape, first, rest, away_first, away_rest = begun
        (across,) = pieces_joined(make, operands, shape, first, away_first)
        to_side = self.send(across[0], y=1)
        to_over = self.send(across[1], x=1)
        side, over, own = pieces_joined(make, operands, shape, rest, away_rest)
        return side, over, to_side, to_over, own

    def narrow(self, joined):
        side, over, to_side, to_over, own = joined
        side = jnp.stack([(side[0].astype(F32) + to_side.astype(F32)).astype(BF), side[1]])
        over = jnp.stack([over[0], (over[1].astype(F32) + to_over.astype(F32)).astype(BF)])
        from_side = self.send(side, x=1)
        from_over = self.send(over, y=1)
        return own.astype(F32) + from_side.astype(F32) + from_over.astype(F32)

    def spread_turned(self, shard):
        shards = [shard] + [self.send(shard, z=k) for k in range(1, self.deep)]
        half = self.deep // 2
        return jnp.stack(
            [jnp.concatenate([t.T for t in shards[h * half : (h + 1) * half]], axis=1) for h in (0, 1)]
        )

    def settle_turned(self, own):
        half = self.deep // 2
        cols = own.shape[2] // half
        cut = [own[k // half][:, (k % half) * cols : (k % half + 1) * cols] for k in range(self.deep)]
        result = cut[0].T
        for k in range(1, self.deep):
            result = result + self.send(cut[k].astype(BF).T, z=k).astype(F32)
        return result

    def settle(self, own):
        rows = own.shape[-2] // self.deep
        cut = [own[..., k * rows : (k + 1) * rows, :] for k in range(self.deep)]
        result = cut[0]
        for k in range(1, self.deep):
            result = result + self.send(cut[k].astype(BF), z=k).astype(F32)
        return result

    def reduce_gains(self, pair):
        total = pair + self.send(pair, c=1)
        total = total + self.send(total, x=1)
        total = total + self.send(total, y=1)
        total = total + sum(self.send(total, z=k) for k in range(1, self.deep))
        width = pair.shape[1] // (2 * self.deep)
        return lax.dynamic_slice_in_dim(total, self.dp * width, width, axis=1)

    def dp_matrix(self, extent):
        width = extent // (2 * self.deep)
        place = jnp.arange(extent, dtype=jnp.int32)
        block, within = place // width, place % width
        ky, kz = block // self.deep, block % self.deep
        source = ((self.z ^ kz) * 2 + (self.y ^ ky)) * width + within
        return (jnp.arange(extent, dtype=jnp.int32)[:, None] == source[None, :]).astype(BF)

    def f_matrix(self, extent):
        width = extent // self.parts
        place = jnp.arange(extent, dtype=jnp.int32)
        source = (self.f ^ (place // width)) * width + place % width
        return (jnp.arange(extent, dtype=jnp.int32)[:, None] == source[None, :]).astype(BF)

def make_plan(mesh):
    dp, parts = mesh.shape["dp"], mesh.shape["fsdp"]
    if parts == 4 and dp == 2 * parts:
        return Paired(mesh)
    return Plain(mesh)


def rotate(heads, cosine, sine):
    half = heads.shape[-1] // 2
    u, w = heads[..., :half], heads[..., half:]
    return jnp.concatenate([u * cosine - w * sine, w * cosine + u * sine], axis=-1)


def unrotate(heads, cosine, sine):
    half = heads.shape[-1] // 2
    u, w = heads[..., :half], heads[..., half:]
    return jnp.concatenate([u * cosine + w * sine, w * cosine - u * sine], axis=-1)


def product(form, a, b):
    return jnp.einsum(form, a, b, preferred_element_type=F32)


def paired_step(plan, tokens, segment_ids, w_query, w_key, w_value, w_output, w_gate, w_up,
                w_down, gain_attn, gain_ffn, out_grad):
    parts = plan.parts
    rows, length = segment_ids.shape
    count, width = tokens.shape
    q_cols, k_cols, o_cols = w_query.shape[1], w_key.shape[1], w_output.shape[1]
    sizes = (o_cols, q_cols, k_cols)
    order = [(f, y) for f in range(parts) for y in range(2)]

    gains = plan.gather_gains(jnp.stack([gain_attn, gain_ffn]))
    attn_own = plan.spread(jnp.concatenate([w_output, w_query, w_key, w_value], axis=1))
    attn_side, attn_over = plan.widen(attn_own)
    down_own = plan.spread_turned(tie(w_down, attn_own))
    attn_across = plan.cross(attn_side, attn_over)
    down_side, down_over = plan.widen(down_own)
    gu_own = plan.spread(tie(jnp.stack([w_gate, w_up]), down_own))
    attn = plan.complete(attn_own, attn_side, attn_over, attn_across)
    attn = [attn[o] for o in order]
    gu_side, gu_over = plan.widen(gu_own)
    down = plan.complete(down_own, down_side, down_over, plan.cross(down_side, down_over))
    down = [down[o] for o in order]
    gate_up = plan.complete(gu_own, gu_side, gu_over, plan.cross(gu_side, gu_over))
    gate_up = [gate_up[o] for o in order]

    place = jnp.stack([plan.z ^ plan.f, plan.y, plan.f]).astype(jnp.int32)
    to_dp = plan.dp_matrix(width)
    to_dp = jnp.stack(jnp.split(to_dp, 4, axis=1))
    to_f = jnp.stack(jnp.split(plan.f_matrix(width), parts, axis=1))
    og_f = jnp.stack([mm(out_grad, to_f[f]).astype(BF) for f in range(parts)])
    seg = segment_ids.reshape(-1)
    row = jnp.arange(count, dtype=jnp.int32) // length
    index = jnp.arange(count, dtype=jnp.int32)
    same_row = row[:, None] == row[None, :]
    same = same_row & (seg[:, None] == seg[None, :])
    allowed = (same & (index[None, :] <= index[:, None])).astype(F32)
    before = same_row & (seg[None, :] < seg[:, None])
    pos = (index % length - jnp.sum(before.astype(jnp.int32), axis=1)).astype(F32)
    half_head = HEAD // 2
    frequency = ROPE_BASE ** (-jnp.arange(half_head, dtype=F32) / half_head)
    angles = pos[:, None] * frequency[None, :]
    cos, sin = jnp.cos(angles), jnp.sin(angles)
    cosine = jnp.concatenate([cos, cos], axis=1)
    sine = jnp.concatenate([-sin, sin], axis=1)

    tall, mid, normed2, *kept = attention_forward(
        place, tokens, gains, cosine, sine, allowed, to_dp, attn, sizes
    )
    act, d_gate, d_up, d_normed2, block_out = feed_forward(
        place, normed2, og_f, mid, down, gate_up
    )

    def gu_piece(refs, f, y, h):
        return jnp.concatenate([t_mm(refs[0][2 * y + i], refs[1 + h][f]) for i in range(2)], axis=0)

    def down_piece(refs, f, y, h):
        return t_mm(refs[0][f], refs[1][y, h])

    def attn_piece(refs, f, y, h):
        return t_mm(refs[0][2 * y + h], refs[1][f])

    gu_sum = plan.start(gu_piece, (normed2, d_gate, d_up), gu_own.shape)
    down_sum = plan.start(down_piece, (og_f, act), down_own.shape)
    gu_sum = plan.join(gu_sum)
    down_sum = plan.join(down_sum)
    d_normed2 = tie(d_normed2, gu_sum[-1], down_sum[-1])
    flat, in_grad, gain_parts = attention_backward(
        place, tokens, gains, cosine, sine, to_dp, to_f, out_grad, mid, d_normed2, kept, attn, sizes
    )
    attn_sum = plan.start(attn_piece, (tall, flat), attn_own.shape)
    gu_sum = plan.narrow(gu_sum)
    down_sum = plan.narrow(down_sum)
    attn_sum = plan.narrow(plan.join(attn_sum))
    grad_gu = plan.settle(gu_sum)
    grad_down = plan.settle_turned(down_sum)
    grad_attn = plan.settle(attn_sum.reshape(-1, attn_sum.shape[2]))
    grad_gains = plan.reduce_gains(gain_parts)
    a, b, c = o_cols, o_cols + q_cols, o_cols + q_cols + k_cols
    return (
        block_out,
        in_grad,
        grad_attn[:, a:b],
        grad_attn[:, b:c],
        grad_attn[:, c:],
        grad_attn[:, :a],
        grad_gu[0],
        grad_gu[1],
        grad_down,
        grad_gains[0],
        grad_gains[1],
    )


def on_device(mesh, tokens, segment_ids, w_query, w_key, w_value, w_output, w_gate, w_up, w_down,
              gain_attn, gain_ffn, out_grad):
    plan = make_plan(mesh)
    if isinstance(plan, Paired):
        return paired_step(plan, tokens, segment_ids, w_query, w_key, w_value, w_output, w_gate,
                           w_up, w_down, gain_attn, gain_ffn, out_grad)
    parts, halves = plan.parts, plan.halves
    rows, length = segment_ids.shape
    count, width = tokens.shape
    q_cols, k_cols, o_cols = w_query.shape[1], w_key.shape[1], w_output.shape[1]
    heads = q_cols * parts // HEAD
    groups = k_cols * parts // HEAD
    per_group = heads // groups
    score_scale = HEAD ** (-0.5)

    gains = plan.gather_gains(jnp.stack([gain_attn, gain_ffn]))
    attn = plan.gather(jnp.concatenate([w_output, w_query, w_key, w_value], axis=1))
    down = plan.gather(w_down)
    gate_w = plan.gather(w_gate)
    up_w = plan.gather(w_up)
    gain_a = gains[0:1].astype(F32)
    gain_f = gains[1:2].astype(F32)

    same = segment_ids[:, :, None] == segment_ids[:, None, :]
    before = segment_ids[:, None, :] < segment_ids[:, :, None]
    index = jnp.arange(length, dtype=jnp.int32)
    pos = (index[None, :] - jnp.sum(before.astype(jnp.int32), axis=-1)).astype(F32)
    half_head = HEAD // 2
    frequency = ROPE_BASE ** (-jnp.arange(half_head, dtype=F32) / half_head)
    angles = pos[:, :, None, None] * frequency
    cosine, sine = jnp.cos(angles), jnp.sin(angles)
    allowed = (same & (index[None, :] <= index[:, None])[None])[:, None, None]

    wide = tokens.astype(F32)
    inv1 = lax.rsqrt(jnp.mean(wide * wide, axis=1, keepdims=True) + EPS)
    normed1 = (wide * inv1 * gain_a).astype(BF)
    normed1_dp = plan.to_dp(normed1)
    mixed = plan.order_f(
        [sum(mm(normed1_dp[y], attn[(f, y)]) for y in range(halves)) for f in range(parts)]
    )
    at = o_cols
    query = jnp.concatenate([m[:, at : at + q_cols] for m in mixed], axis=1)
    at += q_cols
    key = jnp.concatenate([m[:, at : at + k_cols] for m in mixed], axis=1)
    at += k_cols
    value = jnp.concatenate([m[:, at:] for m in mixed], axis=1).astype(BF)
    query = rotate(query.reshape(rows, length, heads, HEAD), cosine, sine).astype(BF)
    query = query.reshape(rows, length, groups, per_group, HEAD)
    key = rotate(key.reshape(rows, length, groups, HEAD), cosine, sine).astype(BF)
    value = value.reshape(rows, length, groups, HEAD)
    scores = product("bsgrd,btgd->bgrst", query, key) * score_scale
    raised = jnp.where(allowed, jnp.exp(scores), 0.0)
    probs = raised / jnp.sum(raised, axis=-1, keepdims=True)
    probs_low = probs.astype(BF)
    attn_in = product("bgrst,btgd->bsgrd", probs_low, value).reshape(count, width).astype(BF)
    attn_in_dp = plan.to_dp(attn_in)
    projected = [
        sum(mm(attn_in_dp[y], attn[(f, y)][:, :o_cols]) for y in range(halves))
        for f in range(parts)
    ]
    mid = wide + plan.from_f(projected)

    inv2 = lax.rsqrt(jnp.mean(mid * mid, axis=1, keepdims=True) + EPS)
    scaled2 = mid * inv2
    normed2 = (scaled2 * gain_f).astype(BF)
    normed2_dp = plan.to_dp(normed2)
    og_f = plan.to_f(out_grad)
    d_act = plan.hidden_from_dp(
        [sum(mm_t(og_f[f], down[(f, y)]) for f in range(parts)) for y in range(halves)]
    )
    acts, d_gate, d_up = [], [], []
    for f in range(parts):
        gate = sum(mm(normed2_dp[y], gate_w[(f, y)]) for y in range(halves))
        upward = sum(mm(normed2_dp[y], up_w[(f, y)]) for y in range(halves))
        sg = jax.nn.sigmoid(gate)
        silu = gate * sg
        acts.append((silu * upward).astype(BF))
        d_gate.append((d_act[f] * upward * sg * (1.0 + gate * (1.0 - sg))).astype(BF))
        d_up.append((d_act[f] * silu).astype(BF))
    act_dp = plan.hidden_to_dp(acts)

    grad_gate = plan.reduce(lambda f, y: t_mm(normed2_dp[y], d_gate[f]))
    grad_up = plan.reduce(lambda f, y: t_mm(normed2_dp[y], d_up[f]))
    grad_down = plan.reduce(lambda f, y: t_mm(act_dp[y], og_f[f]))

    d_normed2 = plan.from_dp(
        [
            sum(mm_t(d_gate[f], gate_w[(f, y)]) + mm_t(d_up[f], up_w[(f, y)]) for f in range(parts))
            for y in range(halves)
        ]
    )
    e2 = d_normed2 * gain_f
    d_mid = out_grad.astype(F32) + inv2 * (
        e2 - scaled2 * jnp.mean(e2 * scaled2, axis=1, keepdims=True)
    )
    d_attn = d_mid.astype(BF)
    d_attn_f = plan.to_f(d_attn)

    d_heads_dp = [
        sum(mm_t(d_attn_f[f], attn[(f, y)][:, :o_cols]) for f in range(parts)).astype(F32)
        for y in range(halves)
    ]
    d_heads = plan.from_dp(d_heads_dp).astype(BF).reshape(rows, length, groups, per_group, HEAD)
    d_value = product("bgrst,bsgrd->btgd", probs_low, d_heads).astype(BF)
    d_probs = product("bsgrd,btgd->bgrst", d_heads, value)
    d_scores = (
        probs * (d_probs - jnp.sum(probs * d_probs, axis=-1, keepdims=True))
    ).astype(BF)
    d_query = product("bgrst,btgd->bsgrd", d_scores, key) * score_scale
    d_query = unrotate(d_query.reshape(rows, length, heads, HEAD), cosine, sine)
    d_query = d_query.astype(BF).reshape(count, heads * HEAD)
    d_key = product("bgrst,bsgrd->btgd", d_scores, query) * score_scale
    d_key = unrotate(d_key, cosine, sine).astype(BF).reshape(count, groups * HEAD)
    d_value = d_value.reshape(count, groups * HEAD)
    blank = jnp.zeros((count, o_cols), BF)
    d_mixed = plan.order_f(
        [
            jnp.concatenate(
                [
                    blank,
                    d_query[:, f * q_cols : (f + 1) * q_cols],
                    d_key[:, f * k_cols : (f + 1) * k_cols],
                    d_value[:, f * k_cols : (f + 1) * k_cols],
                ],
                axis=1,
            )
            for f in range(parts)
        ]
    )
    rest = jnp.zeros((count, q_cols + 2 * k_cols), BF)
    tall = [jnp.concatenate([a, b], axis=0) for a, b in zip(attn_in_dp, normed1_dp)]
    flat = [
        jnp.concatenate([jnp.concatenate([d_attn_f[f], rest], axis=1), d_mixed[f]], axis=0)
        for f in range(parts)
    ]
    grad_attn = plan.reduce(lambda f, y: t_mm(tall[y], flat[f]))
    d_normed1 = plan.from_dp(
        [sum(mm_t(d_mixed[f], attn[(f, y)]) for f in range(parts)) for y in range(halves)]
    )
    scaled1 = wide * inv1
    e1 = d_normed1 * gain_a
    in_grad = d_mid + inv1 * (e1 - scaled1 * jnp.mean(e1 * scaled1, axis=1, keepdims=True))
    grad_gains = plan.reduce_gains(
        jnp.stack([jnp.sum(d_normed1 * scaled1, axis=0), jnp.sum(d_normed2 * scaled2, axis=0)])
    )

    lifted = [
        sum(mm(act_dp[y], down[(f, y)]) for y in range(halves)) for f in range(parts)
    ]
    block_out = (mid + plan.from_f(lifted)).astype(BF)

    a, b, c = o_cols, o_cols + q_cols, o_cols + q_cols + k_cols
    return (
        block_out,
        in_grad,
        grad_attn[:, a:b],
        grad_attn[:, b:c],
        grad_attn[:, c:],
        grad_attn[:, :a],
        grad_gate,
        grad_up,
        grad_down,
        grad_gains[0],
        grad_gains[1],
    )


def solution(mesh):
    token = P(AXES, None)
    matrix = P("dp", "fsdp")
    gain = P("dp")

    def body(*args):
        return on_device(mesh, *args)

    return jax.shard_map(
        body,
        mesh=mesh,
        in_specs=(token, token) + (matrix,) * 7 + (gain, gain, token),
        out_specs=(token, token) + (matrix,) * 7 + (gain, gain),
        check_vma=False,
    )
```
